256 devices in a mesh: tok: 16 (over z, y_hi), feat: 4 (over x), pb: 4 (over y_lo, core).
Axes of the slice: x: 4, y: 4 (y_hi: 2, y_lo: 2; y = y_hi * 2 + y_lo), z: 8, core: 2. Of those that a mesh axis runs over, the one named last changes fastest.
Arguments:
- out_grads: bfloat16 [81920, 8192], P(('tok', 'pb'), 'feat'), may hold values from -6 to 6
- acts: bfloat16 [81920, 8192], P(('tok', 'pb'), 'feat'), may hold values from -6 to 6
- s_inverse: bfloat16 [8192, 8192], P('feat', ('tok', 'pb')), may hold values from -1 to 3, as said below
- a_inverse: bfloat16 [8192, 8192], P('feat', ('tok', 'pb')), may hold values from -1 to 3, as said below
- query_out: bfloat16 [8192, 512], P(('tok', 'pb')), may hold values from -0.0625 to 0.0625
- query_in: bfloat16 [8192, 512], P(('tok', 'pb')), may hold values from -0.0625 to 0.0625
Outputs:
- scores: float32 [32, 81920], P('feat', ('tok', 'pb'))
The draws below stay inside these ranges and needn't reach their ends.
Inputs may be any that keep to these rules, and one draw needn't show every extreme that they name: `s_inverse`: symmetric; diagonal entries roughly between 0.5 and 2. `a_inverse`: symmetric; diagonal entries roughly between 0.5 and 2.
All inputs are finite; a program needn't handle non-finite values.
Results may differ from the reference program's by a relative error of at most 0.0041.
Values may be sent and summed in bfloat16 or wider, within the bound.
A program may use at most 128 MiB of HBM per device.

```python
import jax
import jax.numpy as jnp
from jax import lax

D = 8192
RANK = 16
QUERIES = 32
TOK_DEV = 1280
QR = 512
TOKENS = 81920


def factor_draw(key):
    first, second = jax.random.split(key)
    diag_vals = jnp.exp(jax.random.uniform(first, (D,), jnp.float32, jnp.log(0.5), jnp.log(2.0)))
    noise = jax.random.normal(second, (D, D), jnp.float32)
    symmetric = (noise + noise.T) * (0.25 / D ** 0.5)
    return (jnp.diag(diag_vals) + symmetric).astype(jnp.bfloat16)


def draw_s_inverse(key, part):
    return factor_draw(jax.random.fold_in(key, 11))


def draw_a_inverse(key, part):
    return factor_draw(jax.random.fold_in(key, 23))


def level_of(key, extent, pieces, low, high):
    factor_of = 1.0
    for axis_at, parts in pieces:
        steps = jax.random.uniform(jax.random.fold_in(jax.random.fold_in(key, 6), axis_at), (parts,), jnp.float32, low / len(pieces), high / len(pieces))
        factor_of = factor_of * jnp.repeat(jnp.exp(steps), extent[axis_at] // parts).reshape((-1,) + (1,) * (len(extent) - 1 - axis_at))
    return factor_of


def bell_draw(own_key, shape, width, reach, cuts=(), dtype=jnp.bfloat16):
    drawn = jax.random.normal(own_key, shape, jnp.float32) * width
    if len(cuts) > 0:
        drawn = level_of(own_key, shape, cuts, -0.22, 0.18) * drawn
    return jnp.clip(drawn, min=-reach, max=reach).astype(dtype)


def setup_inputs(seed: int = 0) -> dict:
    key_list = jax.random.split(jax.random.key(seed), 7)
    out_grads = bell_draw(key_list[0], (TOKENS, D), 1.0, 6.0, ((0, 64), (1, 4)))
    acts = bell_draw(key_list[1], (TOKENS, D), 1.0, 6.0, ((0, 64), (1, 4)))
    s_inverse = draw_s_inverse(jax.random.fold_in(key_list[6], 71), 0)
    a_inverse = draw_a_inverse(jax.random.fold_in(key_list[6], 71), 0)
    query_out = bell_draw(key_list[4], (D, QR), D ** -0.5, 0.0625, ((0, 64),))
    query_in = bell_draw(key_list[5], (D, QR), D ** -0.5, 0.0625, ((0, 64),))
    return dict(out_grads=out_grads, acts=acts, s_inverse=s_inverse, a_inverse=a_inverse, query_out=query_out, query_in=query_in)


def reference(out_grads, acts, s_inverse, a_inverse, query_out, query_in):
    left_pre = jnp.dot(s_inverse, query_out, preferred_element_type=jnp.float32).astype(jnp.bfloat16)
    right_pre = jnp.dot(a_inverse, query_in, preferred_element_type=jnp.float32).astype(jnp.bfloat16)
    scale = 1.0 / (RANK ** 0.5)

    def one_block(pair):
        grads, inputs = pair
        grad_proj = jnp.dot(grads, left_pre, preferred_element_type=jnp.float32)
        act_proj = jnp.dot(inputs, right_pre, preferred_element_type=jnp.float32)
        summed = (grad_proj * act_proj).reshape(grads.shape[0], QUERIES, RANK).sum(axis=2)
        return (summed * scale).T

    grads_all = out_grads.reshape(-1, TOK_DEV, D)
    inputs_all = acts.reshape(-1, TOK_DEV, D)
    blocks = lax.map(one_block, (grads_all, inputs_all))
    return jnp.transpose(blocks, (1, 0, 2)).reshape(QUERIES, TOKENS)
```

```python
import functools

import jax
import jax.numpy as jnp
from jax import lax
from jax.experimental import pallas as pl
from jax.experimental.pallas import tpu as pltpu
from jax.sharding import PartitionSpec as P

RANK = 16
MESH = pl.DeviceIdType.MESH
BF16, F32 = jnp.bfloat16, jnp.float32
ROWS = 1280
HALF = ROWS // 2
TILE = 320


def place(x, y, z, k):
    return (z * 2 + lax.div(y, 2), x, lax.rem(y, 2) * 2 + k)


def kernel(
    grads, acts, s_inv, a_inv, q_out, q_in, out,
    xv, mbuf, mt, qv, qrel, qg, part, cbuf, lq, both, own, opp, near, hrecv, frecv,
    l_sem, m_send, m_recv, a_send, a_recv, b_send, b_recv, c_send, c_recv,
    d_send, d_recv, e_send, e_recv, f_send, f_recv, h_send, h_recv, n_send, n_recv,
):
    tok, x, pb = lax.axis_index("tok"), lax.axis_index("feat"), lax.axis_index("pb")
    z, k = lax.div(tok, 2), lax.rem(pb, 2)
    y = lax.rem(tok, 2) * 2 + lax.div(pb, 2)
    home, z2 = lax.div(z, 2), lax.rem(z, 2)
    at_home = home == x

    def xs(d):
        return lax.rem(x + d, 4)

    def ys(d):
        return lax.rem(y + d, 4)

    x_dev = [None] + [place(xs(d), y, z, k) for d in (1, 2, 3)]
    y_dev = [None] + [place(x, ys(d), z, k) for d in (1, 2, 3)]
    twin = place(x, y, z, 1 - k)

    def local(src, dst, sem):
        return pltpu.make_async_copy(src, dst, sem)

    def remote(src, dst, send, recv, dev):
        return pltpu.make_async_remote_copy(
            src_ref=src, dst_ref=dst, send_sem=send, recv_sem=recv,
            device_id=dev, device_id_type=MESH,
        )

    q_rows = pl.ds(pl.multiple_of(x * 32, 32), 32)
    load_q = [local(q.at[q_rows, :], qv.at[m], l_sem.at[m]) for m, q in enumerate((q_out, q_in))]
    for c in load_q:
        c.start()

    @pl.when(k == 0)
    def _():
        local(s_inv, mbuf.at[0], l_sem.at[2]).start()

    @pl.when(k == 1)
    def _():
        local(a_inv, mbuf.at[1], l_sem.at[2]).start()

    load_x = [local(t, xv.at[m], l_sem.at[3 + m]) for m, t in enumerate((grads, acts))]
    for c in load_x:
        c.start()

    barrier = pltpu.get_barrier_semaphore()

    def greet(dev):
        pl.semaphore_signal(barrier, inc=1, device_id=dev, device_id_type=MESH)

    def greet_source(i, carry):
        sx, sz, sk = lax.div(i, 4), 2 * x + lax.rem(lax.div(i, 2), 2), lax.rem(i, 2)
        me = (sx == x) & (sz == z) & (sk == k)

        @pl.when(jnp.logical_not(me))
        def _():
            greet(place(sx, y, sz, sk))

        return carry

    lax.fori_loop(0, 16, greet_source, 0)
    for dev in (y_dev[1], y_dev[3], x_dev[1], x_dev[2], x_dev[3], twin):
        greet(dev)
    pl.semaphore_wait(barrier, 22 - at_home.astype(jnp.int32))

    @pl.when(k == 0)
    def _():
        remote(a_inv, mbuf.at[0], m_send, m_recv, twin).start()

    @pl.when(k == 1)
    def _():
        remote(s_inv, mbuf.at[1], m_send, m_recv, twin).start()

    for c in load_q:
        c.wait()
    for m in range(2):
        for plane in range(4):
            for j, d in enumerate((2, 0, 1, 3)):
                col = (plane + d) % 4 * 128
                qrel[m, plane, :, 128 * j:128 * j + 128] = qv[m, :, col:col + 128]

    q_dst_rows = pl.ds(pl.multiple_of(k * 128 + x * 32, 32), 32)

    def a_copy(h, i):
        zt, kt = lax.rem(z + 4 + lax.div(i, 2), 8), lax.rem(i, 2)
        me = at_home & (zt == z) & (kt == k)
        src = qrel.at[kt, lax.div(zt, 2), :, pl.ds(256 * h, 256)]
        dst = qg.at[h, z2, y, q_dst_rows, :]
        far = remote(src, dst, a_send.at[h, i], a_recv.at[h], place(home, y, zt, kt))
        return me, local(src, dst, a_recv.at[h]), far

    for h in range(2):
        def a_start(i, carry, h=h):
            me, near_copy, far = a_copy(h, i)

            @pl.when(me)
            def _():
                near_copy.start()

            @pl.when(jnp.logical_not(me))
            def _():
                far.start()

            return carry

        lax.fori_loop(0, 16, a_start, 0)

    local(mbuf.at[k], mbuf.at[k], l_sem.at[2]).wait()
    mt[pl.ds(pl.multiple_of(k * 128, 128), 128), :] = mbuf[k].T
    remote(mbuf.at[1 - k], mbuf.at[1 - k], m_send, m_recv, twin).wait_recv()
    mt[pl.ds(pl.multiple_of((1 - k) * 128, 128), 128), :] = mbuf[1 - k].T

    def spread(buf, h, send, recv):
        mine = buf.at[h, :, y]
        up = remote(mine, mine, send.at[h, 0], recv.at[h, 0], y_dev[1])
        down = remote(mine, mine, send.at[h, 1], recv.at[h, 1], y_dev[3])
        up.start()
        down.start()
        return [up, down]

    def landed(buf, h, recv, side):
        block = buf.at[h, :, ys(3) if side == 0 else ys(1)]
        remote(block, block, recv.at[h, side], recv.at[h, side], y_dev[1]).wait_recv()

    def pass_on(buf, h, send, recv, side):
        half = buf.at[h, side, ys(3) if side == 0 else ys(1)]
        c = remote(half, half, send.at[h, 2 + side], recv.at[h, 2 + side],
                   y_dev[1] if side == 0 else y_dev[3])
        c.start()
        return c

    def landed_far(buf, h, recv, side):
        half = buf.at[h, side, ys(2)]
        remote(half, half, recv.at[h, 2 + side], recv.at[h, 2 + side], y_dev[1]).wait_recv()

    sent = []
    for h in range(2):
        block = qg.at[h, :, y]
        local(block, block, a_recv.at[h]).wait()
        sent += spread(qg, h, b_send, b_recv)

    for h in range(2):
        for side in range(2):
            landed(qg, h, b_recv, side)
            sent.append(pass_on(qg, h, b_send, b_recv, side))
        for side in range(2):
            landed_far(qg, h, b_recv, side)
        part[h] = jnp.dot(mt[...], qg[h].reshape(2048, 256), preferred_element_type=F32)
        for d in (1, 2, 3):
            rows = pl.ds(pl.multiple_of(xs(d) * 64, 64), 64)
            c = remote(part.at[h, rows, :], cbuf.at[h, d - 1], c_send.at[h, d - 1],
                       c_recv.at[h, d - 1], x_dev[d])
            c.start()
            sent.append(c)

    mine64 = pl.ds(pl.multiple_of(x * 64, 64), 64)
    mb = both.at[k]

    def d_copy(h, i):
        zt = lax.rem(z + 4 + i, 8)
        me = at_home & (zt == z)
        dst = mb.at[h, z2, y, mine64, :]
        far = remote(lq.at[h], dst, d_send.at[h, i], d_recv.at[h], place(home, y, zt, k))
        return me, local(lq.at[h], dst, d_recv.at[h]), far

    for h in range(2):
        for d in range(3):
            c = cbuf.at[h, d]
            remote(c, c, c_recv.at[h, d], c_recv.at[h, d], x_dev[1]).wait_recv()
        total = part[h, mine64, :] + cbuf[h, 0] + cbuf[h, 1] + cbuf[h, 2]
        lq[h] = total.astype(BF16)

        def d_start(i, carry, h=h):
            me, near_copy, far = d_copy(h, i)

            @pl.when(me)
            def _():
                near_copy.start()

            @pl.when(jnp.logical_not(me))
            def _():
                far.start()

            return carry

        lax.fori_loop(0, 8, d_start, 0)

    def to_twin(h, b):
        block = mb.at[h, :, ys(b)]
        c = remote(block, block, f_send.at[h, b], f_recv.at[h, b], twin)
        c.start()
        sent.append(c)

    for h in range(2):
        block = mb.at[h, :, y]
        local(block, block, d_recv.at[h]).wait()
        sent.extend(spread(mb, h, e_send, e_recv))
        to_twin(h, 0)

    def gather_block(h):
        for side in range(2):
            landed(mb, h, e_recv, side)
            sent.append(pass_on(mb, h, e_send, e_recv, side))
            to_twin(h, 3 if side == 0 else 1)
        for side in range(2):
            landed_far(mb, h, e_recv, side)
        to_twin(h, 2)

    def twin_block(h):
        for b in range(4):
            block = both.at[1 - k, h, :, ys(b)]
            remote(block, block, f_recv.at[h, b], f_recv.at[h, b], twin).wait_recv()

    def project(m, h, tile):
        rows = pl.ds(pl.multiple_of(tile * TILE, TILE), TILE)
        w = both[m, h].reshape(2048, 256)
        return rows, jnp.dot(xv[m, rows, :], w, preferred_element_type=F32)

    gather_block(0)
    for turn in range(2):
        m = k if turn == 0 else 1 - k
        if turn == 0:
            for c in load_x:
                c.wait()
        else:
            twin_block(0)

        def first(tile, carry, m=m):
            rows, acc = project(m, 0, tile)
            opp[m, rows, :] = acc[:, :128].astype(BF16)
            own[m, rows, :] = acc[:, 128:]
            return carry

        lax.fori_loop(0, 4, first, 0)
        for side, d in ((0, 1), (1, 3)):
            c = remote(opp.at[m, pl.ds(HALF * (1 - side), HALF), :], hrecv.at[side, m],
                       h_send.at[turn, side], h_recv.at[m, side], x_dev[d])
            c.start()
            sent.append(c)

    gather_block(1)
    for turn in range(2):
        m = k if turn == 0 else 1 - k
        if turn == 1:
            twin_block(1)
        for side in range(2):
            c = hrecv.at[side, m]
            remote(c, c, h_recv.at[m, side], h_recv.at[m, side], x_dev[1]).wait_recv()
        for part_at in range(2):
            def second(tile, carry, m=m, part_at=part_at):
                rows, acc = project(m, 1, tile + 2 * part_at)
                inner = pl.ds(pl.multiple_of(tile * TILE, TILE), TILE)
                side = 1 - part_at
                more = hrecv[side, m, inner, :].astype(F32)
                for j in range(2):
                    piece = acc[:, 128 * j:128 * j + 128]
                    if j == side:
                        piece = piece + more
                    near[j, m, rows, :] = piece.astype(BF16)
                return carry

            lax.fori_loop(0, 2, second, 0)
            rows = pl.ds(HALF * part_at, HALF)
            for j, d in ((0, 1), (1, 3)):
                c = remote(near.at[j, m, rows, :], frecv.at[j, m, rows, :],
                           n_send.at[turn, part_at, j], n_recv.at[m, part_at, j], x_dev[d])
                c.start()
                sent.append(c)

    lane = lax.broadcasted_iota(jnp.int32, (8, 128), 1)
    query = lax.broadcasted_iota(jnp.int32, (8, 128), 0)
    pick = jnp.where(lax.div(lane, RANK) == query, 1.0, 0.0).astype(F32)
    for part_at in range(2):
        rows = pl.ds(HALF * part_at, HALF)
        for m in range(2):
            for j in range(2):
                c = frecv.at[j, m, rows, :]
                remote(c, c, n_recv.at[m, part_at, j], n_recv.at[m, part_at, j], x_dev[1]).wait_recv()
        g, a = (own[m, rows, :] + frecv[0, m, rows, :].astype(F32) + frecv[1, m, rows, :].astype(F32)
                for m in range(2))
        prod = g * a * (1.0 / RANK**0.5)
        out[:, rows] = lax.dot_general(
            pick, prod, (((1,), (1,)), ((), ())),
            precision=lax.Precision.HIGHEST, preferred_element_type=F32,
        )

    for c in sent:
        c.wait_send()
    remote(mbuf.at[k], mbuf.at[k], m_send, m_recv, twin).wait_send()
    for h in range(2):
        def a_sent(i, carry, h=h):
            me, _, far = a_copy(h, i)

            @pl.when(jnp.logical_not(me))
            def _():
                far.wait_send()

            return carry

        lax.fori_loop(0, 16, a_sent, 0)

        def d_sent(i, carry, h=h):
            me, _, far = d_copy(h, i)

            @pl.when(jnp.logical_not(me))
            def _():
                far.wait_send()

            return carry

        lax.fori_loop(0, 8, d_sent, 0)


def per_device(out_grads, acts, s_inverse, a_inverse, query_out, query_in):
    dma = pltpu.SemaphoreType.DMA
    vmem = pltpu.VMEM
    return pl.pallas_call(
        kernel,
        out_shape=jax.ShapeDtypeStruct((8, ROWS), F32),
        in_specs=[pl.BlockSpec(memory_space=pl.ANY)] * 6,
        out_specs=pl.BlockSpec(memory_space=pltpu.VMEM),
        scratch_shapes=[
            vmem((2, ROWS, 2048), BF16),
            vmem((2, 2048, 128), BF16),
            vmem((256, 2048), BF16),
            vmem((2, 32, 512), BF16),
            vmem((2, 4, 32, 512), BF16),
            vmem((2, 2, 4, 256, 256), BF16),
            vmem((2, 256, 256), F32),
            vmem((2, 3, 64, 256), F32),
            vmem((2, 64, 256), BF16),
            vmem((2, 2, 2, 4, 256, 256), BF16),
            vmem((2, ROWS, 128), F32),
            vmem((2, ROWS, 128), BF16),
            vmem((2, 2, ROWS, 128), BF16),
            vmem((2, 2, HALF, 128), BF16),
            vmem((2, 2, ROWS, 128), BF16),
            dma((5,)), dma, dma, dma((2, 16)), dma((2,)), dma((2, 4)), dma((2, 4)),
            dma((2, 3)), dma((2, 3)), dma((2, 8)), dma((2,)), dma((2, 4)), dma((2, 4)),
            dma((2, 4)), dma((2, 4)), dma((2, 2)), dma((2, 2)), dma((2, 2, 2)), dma((2, 2, 2)),
        ],
        compiler_params=pltpu.CompilerParams(
            collective_id=0, has_side_effects=True, vmem_limit_bytes=52 * 1024 * 1024
        ),
    )(out_grads, acts, s_inverse, a_inverse, query_out, query_in)


def solution(mesh):
    placed = (
        P(("tok", "pb"), "feat"),
        P(("tok", "pb"), "feat"),
        P("feat", ("tok", "pb")),
        P("feat", ("tok", "pb")),
        P(("tok", "pb"), None),
        P(("tok", "pb"), None),
    )
    return jax.shard_map(
        per_device, mesh=mesh, in_specs=placed, out_specs=P("feat", ("tok", "pb")), check_vma=False
    )
```

```python
import jax
import jax.numpy as jnp
from jax import lax
from jax.experimental import pallas as pl
from jax.experimental.pallas import tpu as pltpu
from jax.sharding import PartitionSpec as P

RANK = 16
MESH = pl.DeviceIdType.MESH
BF16, F32 = jnp.bfloat16, jnp.float32
ROWS = 1280
HALF = ROWS // 2
TILE = 320


def place(x, y, z, k):
    return (z * 2 + lax.div(y, 2), x, lax.rem(y, 2) * 2 + k)


def kernel(
    grads, acts, s_inv, a_inv, q_out, q_in, out,
    xv, mbuf, mt, qv, qrel, qg, part, cbuf, lq, both, own, opp, near, hrecv, frecv, pend,
    l_sem, m_send, m_recv, a_send, a_recv, b_send, b_recv, c_send, c_recv,
    d_send, d_recv, e_send, e_recv, f_send, f_recv, h_send, h_recv, n_send, n_recv,
):
    tok, x, pb = lax.axis_index("tok"), lax.axis_index("feat"), lax.axis_index("pb")
    z, k = lax.div(tok, 2), lax.rem(pb, 2)
    y = lax.rem(tok, 2) * 2 + lax.div(pb, 2)
    home, z2 = lax.div(z, 2), lax.rem(z, 2)
    at_home = home == x

    def xs(d):
        return lax.rem(x + d, 4)

    def ys(d):
        return lax.rem(y + d, 4)

    x_dev = [None] + [place(xs(d), y, z, k) for d in (1, 2, 3)]
    y_dev = [None] + [place(x, ys(d), z, k) for d in (1, 2, 3)]
    twin = place(x, y, z, 1 - k)

    def local(src, dst, sem):
        return pltpu.make_async_copy(src, dst, sem)

    def remote(src, dst, send, recv, dev):
        return pltpu.make_async_remote_copy(
            src_ref=src, dst_ref=dst, send_sem=send, recv_sem=recv,
            device_id=dev, device_id_type=MESH,
        )

    sent = []

    def arrived(ref, sem):
        local(ref, ref, sem).wait()

    q_rows = pl.ds(pl.multiple_of(x * 32, 32), 32)
    load_q = [local(q.at[q_rows, :], qv.at[m], l_sem.at[m]) for m, q in enumerate((q_out, q_in))]
    for c in load_q:
        c.start()

    @pl.when(k == 0)
    def _():
        local(s_inv, mbuf.at[0], l_sem.at[2]).start()

    @pl.when(k == 1)
    def _():
        local(a_inv, mbuf.at[1], l_sem.at[2]).start()

    load_x = [local(t, xv.at[m], l_sem.at[3 + m]) for m, t in enumerate((grads, acts))]
    for c in load_x:
        c.start()

    barrier = pltpu.get_barrier_semaphore()

    def greet(dev):
        pl.semaphore_signal(barrier, inc=1, device_id=dev, device_id_type=MESH)

    def greet_source(i, carry):
        sx, sz, sk = lax.div(i, 4), 2 * x + lax.rem(lax.div(i, 2), 2), lax.rem(i, 2)
        me = (sx == x) & (sz == z) & (sk == k)

        @pl.when(jnp.logical_not(me))
        def _():
            greet(place(sx, y, sz, sk))

        return carry

    lax.fori_loop(0, 16, greet_source, 0)
    for dev in (y_dev[1], y_dev[3], x_dev[1], x_dev[2], x_dev[3], twin):
        greet(dev)

    lane = lax.broadcasted_iota(jnp.int32, (8, 128), 1)
    low = lax.broadcasted_iota(jnp.int32, (1, 128), 1) < 64

    def join(a, b):
        return jnp.where(low, a, b)

    def flip(a):
        return pltpu.roll(a, 64, 1)

    for c in load_q:
        c.wait()
    for m in range(2):
        for plane in range(4):
            col = [(plane + d) % 4 * 128 for d in range(4)]
            up, down = (qv[m, :, col[d]:col[d] + 128].astype(F32) for d in (1, 3))
            qrel[m, plane, 0] = qv[m, :, col[2]:col[2] + 128]
            qrel[m, plane, 1] = join(up, flip(down)).astype(BF16)
            qrel[m, plane, 2] = join(flip(up), down).astype(BF16)
            qrel[m, plane, 3] = qv[m, :, col[0]:col[0] + 128]

    arrived(mbuf.at[k], l_sem.at[2])
    mt[pl.ds(pl.multiple_of(k * 128, 128), 128), :] = mbuf[k].T
    pl.semaphore_wait(barrier, 22 - at_home.astype(jnp.int32))

    @pl.when(k == 0)
    def _():
        remote(a_inv, mbuf.at[0], m_send, m_recv, twin).start()

    @pl.when(k == 1)
    def _():
        remote(s_inv, mbuf.at[1], m_send, m_recv, twin).start()

    q_dst_rows = pl.ds(pl.multiple_of(k * 128 + x * 32, 32), 32)
    mine64 = pl.ds(pl.multiple_of(x * 64, 64), 64)
    mb = both.at[k]

    def ship(src, dst, send, recv, dev):
        c = remote(src, dst, send, recv, dev)
        c.start()
        sent.append(c)

    def a_copy(p, i):
        zt, kt = lax.rem(z + 4 + lax.div(i, 2), 8), lax.rem(i, 2)
        me = at_home & (zt == z) & (kt == k)
        src = qrel.at[kt, lax.div(zt, 2), p]
        dst = qg.at[p, z2, y, q_dst_rows, :]
        far = remote(src, dst, a_send.at[p, i], a_recv.at[p], place(home, y, zt, kt))
        return me, local(src, dst, a_recv.at[p]), far

    def d_copy(p, i):
        zt = lax.rem(z + 4 + i, 8)
        me = at_home & (zt == z)
        dst = mb.at[p, z2, y, mine64, :]
        far = remote(lq.at[p], dst, d_send.at[p, i], d_recv.at[p], place(home, y, zt, k))
        return me, local(lq.at[p], dst, d_recv.at[p]), far

    def fan_start(copy, count, p):
        def step(i, carry):
            me, near_copy, far = copy(p, i)

            @pl.when(me)
            def _():
                near_copy.start()

            @pl.when(jnp.logical_not(me))
            def _():
                far.start()

            return carry

        lax.fori_loop(0, count, step, 0)

    def fan_sent(copy, count, p):
        def step(i, carry):
            me, _, far = copy(p, i)

            @pl.when(jnp.logical_not(me))
            def _():
                far.wait_send()

            return carry

        lax.fori_loop(0, count, step, 0)

    def spread(buf, p, send, recv):
        for half, side, d in ((0, 0, 1), (1, 1, 3), (1, 0, 1), (0, 1, 3)):
            mine = buf.at[p, half, y]
            ship(mine, mine, send.at[p, side, half], recv.at[p, side, half], y_dev[d])

    def near_half(buf, p, recv, side, half):
        b = ys(3) if side == 0 else ys(1)
        arrived(buf.at[p, half, b], recv.at[p, side, half])

    def pass_on(buf, p, send, recv):
        for side, d in ((0, 1), (1, 3)):
            near_half(buf, p, recv, side, side)
            half = buf.at[p, side, ys(3) if side == 0 else ys(1)]
            ship(half, half, send.at[p, 2, side], recv.at[p, 2, side], y_dev[d])

    def far_half(buf, p, recv, side):
        arrived(buf.at[p, side, ys(2)], recv.at[p, 2, side])

    def to_twin(p, b, half):
        block = mb.at[p, half, ys(b)]
        ship(block, block, f_send.at[p, b, half], f_recv.at[p, b, half], twin)

    def A(p):
        fan_start(a_copy, 16, p)

    def A_sent(p):
        fan_sent(a_copy, 16, p)

    def B(p):
        arrived(qg.at[p, :, y], a_recv.at[p])
        spread(qg, p, b_send, b_recv)

    def B2(p):
        pass_on(qg, p, b_send, b_recv)

    def C(p):
        for side in range(2):
            near_half(qg, p, b_recv, side, 1 - side)
            far_half(qg, p, b_recv, side)
        part[p] = jnp.dot(mt[...], qg[p].reshape(2048, 128), preferred_element_type=F32)
        for d in (1, 2, 3):
            rows = pl.ds(pl.multiple_of(xs(d) * 64, 64), 64)
            ship(part.at[p, rows, :], cbuf.at[p, d - 1], c_send.at[p, d - 1],
                 c_recv.at[p, d - 1], x_dev[d])

    def D(p):
        for d in range(3):
            arrived(cbuf.at[p, d], c_recv.at[p, d])
        total = part[p, mine64, :] + cbuf[p, 0] + cbuf[p, 1] + cbuf[p, 2]
        lq[p] = total.astype(BF16)
        fan_start(d_copy, 8, p)

    def E(p):
        arrived(mb.at[p, :, y], d_recv.at[p])
        spread(mb, p, e_send, e_recv)
        to_twin(p, 0, 0)
        to_twin(p, 0, 1)

    def E2(p):
        pass_on(mb, p, e_send, e_recv)
        to_twin(p, 3, 0)
        to_twin(p, 1, 1)

    def E3(p):
        for side in range(2):
            near_half(mb, p, e_recv, side, 1 - side)
            to_twin(p, 3 if side == 0 else 1, 1 - side)
        for side in range(2):
            far_half(mb, p, e_recv, side)
            to_twin(p, 2, side)

    def factor():
        c = 1 - k
        arrived(mbuf.at[c], m_recv)
        mt[pl.ds(pl.multiple_of(c * 128, 128), 128), :] = mbuf[c].T

    def acts_in():
        for c in load_x:
            c.wait()

    def twin_in(p):
        for b in range(4):
            for half in range(2):
                arrived(both.at[1 - k, p, half, ys(b)], f_recv.at[p, b, half])

    def tiles(half, body):
        def step(i, carry):
            rows = pl.ds(pl.multiple_of((i + half * (HALF // TILE)) * TILE, TILE), TILE)
            body(rows, pl.ds(pl.multiple_of(i * TILE, TILE), TILE))
            return carry

        lax.fori_loop(0, HALF // TILE, step, 0)

    def project(p, m, rows):
        w = both[m, p].reshape(2048, 128)
        return jnp.dot(xv[m, rows, :], w, preferred_element_type=F32)

    def sides(turn):
        return k if turn == 0 else 1 - k

    def H0(turn):
        m = sides(turn)
        for half in range(2):
            def body(rows, inner):
                opp[m, rows, :] = project(0, m, rows).astype(BF16)

            tiles(half, body)
            side, d = ((1, 3), (0, 1))[half]
            ship(opp.at[m, pl.ds(HALF * half, HALF), :], hrecv.at[side, m],
                 h_send.at[turn, side], h_recv.at[m, side], x_dev[d])

    def to_neighbour(s, half, j):
        rows = pl.ds(HALF * half, HALF)
        ship(near.at[j, s, rows, :], frecv.at[j, s, rows, :], n_send.at[s, half, j],
             n_recv.at[s, half, j], x_dev[1 if j == 0 else 3])

    def H1(s, half):
        def body(rows, inner):
            g, a = (project(s + 1, m, rows) for m in range(2))
            both_ways = join(g, flip(a)), join(flip(g), a)
            near[half, s, rows, :] = both_ways[half].astype(BF16)
            pend[s, half, inner, :] = both_ways[1 - half]

        tiles(half, body)
        to_neighbour(s, half, half)

    def H2(s, half):
        j = 1 - half
        if s == 0:
            for m in range(2):
                arrived(hrecv.at[j, m], h_recv.at[m, j])

        def body(rows, inner):
            g, a = (hrecv[j, m, inner, :].astype(F32) for m in range(2))
            more = join(g, flip(a)) if s == 0 else join(flip(g), a)
            near[j, s, rows, :] = (pend[s, half, inner, :] + more).astype(BF16)

        tiles(half, body)
        to_neighbour(s, half, j)

    def H3(turn):
        m = sides(turn)
        for half in range(2):
            def body(rows, inner):
                own[m, rows, :] = project(3, m, rows)

            tiles(half, body)

    query = lax.broadcasted_iota(jnp.int32, (8, 128), 0)
    pick = jnp.where(lax.div(lane, RANK) == query, 1.0, 0.0).astype(F32)

    def scores(half):
        rows = pl.ds(HALF * half, HALF)
        for s in range(2):
            for j in range(2):
                arrived(frecv.at[j, s, rows, :], n_recv.at[s, half, j])
        first, last = (frecv[0, s, rows, :].astype(F32) + frecv[1, s, rows, :].astype(F32)
                       for s in range(2))
        g = own[0, rows, :] + join(first, flip(last))
        a = own[1, rows, :] + join(flip(first), last)
        prod = g * a * (1.0 / RANK**0.5)
        out[:, rows] = lax.dot_general(
            pick, prod, (((1,), (1,)), ((), ())),
            precision=lax.Precision.HIGHEST, preferred_element_type=F32,
        )

    A(0)
    A(1)
    factor()
    B(0)
    A(2)
    B(1)
    A(3)
    B2(0)
    B(2)
    C(0)
    B2(1)
    B(3)
    D(0)
    C(1)
    B2(2)
    D(1)
    E(0)
    C(2)
    B2(3)
    E2(0)
    D(2)
    E(1)
    C(3)
    E3(0)
    acts_in()
    H0(0)
    E2(1)
    twin_in(0)
    H0(1)
    E(2)
    D(3)
    E3(1)
    twin_in(1)
    H1(0,0)
    E2(2)
    H1(0,1)
    E(3)
    H2(0,0)
    H2(0,1)
    E3(2)
    twin_in(2)
    H1(1,0)
    H1(1,1)
    E2(3)
    H2(1,0)
    H2(1,1)
    E3(3)
    H3(0)
    twin_in(3)
    H3(1)
    scores(0)
    scores(1)

    for c in sent:
        c.wait_send()
    remote(mbuf.at[k], mbuf.at[k], m_send, m_recv, twin).wait_send()
    for p in range(4):
        fan_sent(a_copy, 16, p)
        fan_sent(d_copy, 8, p)


def per_device(out_grads, acts, s_inverse, a_inverse, query_out, query_in):
    dma = pltpu.SemaphoreType.DMA
    vmem = pltpu.VMEM
    return pl.pallas_call(
        kernel,
        out_shape=jax.ShapeDtypeStruct((8, ROWS), F32),
        in_specs=[pl.BlockSpec(memory_space=pl.ANY)] * 6,
        out_specs=pl.BlockSpec(memory_space=pltpu.VMEM),
        scratch_shapes=[
            vmem((2, ROWS, 2048), BF16),
            vmem((2, 2048, 128), BF16),
            vmem((256, 2048), BF16),
            vmem((2, 32, 512), BF16),
            vmem((2, 4, 4, 32, 128), BF16),
            vmem((4, 2, 4, 256, 128), BF16),
            vmem((4, 256, 128), F32),
            vmem((4, 3, 64, 128), F32),
            vmem((4, 64, 128), BF16),
            vmem((2, 4, 2, 4, 256, 128), BF16),
            vmem((2, ROWS, 128), F32),
            vmem((2, ROWS, 128), BF16),
            vmem((2, 2, ROWS, 128), BF16),
            vmem((2, 2, HALF, 128), BF16),
            vmem((2, 2, ROWS, 128), BF16),
            vmem((2, 2, HALF, 128), F32),
            dma((5,)), dma, dma, dma((4, 16)), dma((4,)), dma((4, 3, 2)), dma((4, 3, 2)),
            dma((4, 3)), dma((4, 3)), dma((4, 8)), dma((4,)), dma((4, 3, 2)), dma((4, 3, 2)),
            dma((4, 4, 2)), dma((4, 4, 2)), dma((2, 2)), dma((2, 2)), dma((2, 2, 2)), dma((2, 2, 2)),
        ],
        compiler_params=pltpu.CompilerParams(
            collective_id=0, has_side_effects=True, vmem_limit_bytes=62 * 1024 * 1024
        ),
    )(out_grads, acts, s_inverse, a_inverse, query_out, query_in)


def solution(mesh):
    placed = (
        P(("tok", "pb"), "feat"),
        P(("tok", "pb"), "feat"),
        P("feat", ("tok", "pb")),
        P("feat", ("tok", "pb")),
        P(("tok", "pb"), None),
        P(("tok", "pb"), None),
    )
    return jax.shard_map(
        per_device, mesh=mesh, in_specs=placed, out_specs=P("feat", ("tok", "pb")), check_vma=False
    )
```

```python
import jax
import jax.numpy as jnp
from jax import lax
from jax.experimental import pallas as pl
from jax.experimental.pallas import tpu as pltpu
from jax.sharding import PartitionSpec as P

RANK = 16
MESH = pl.DeviceIdType.MESH
BF16, F32 = jnp.bfloat16, jnp.float32
ROWS = 1280
HALF = ROWS // 2
TILE = 640


def place(x, y, z, k):
    return (z * 2 + lax.div(y, 2), x, lax.rem(y, 2) * 2 + k)


def kernel(
    grads, acts, s_inv, a_inv, q_out, q_in, out,
    xv, mbuf, mt, qv, qrel, qg, part, cbuf, lq, both, own, opp, near, hrecv, frecv, pend,
    l_sem, m_send, m_recv, a_send, a_recv, b_send, b_recv, c_send, c_recv,
    d_send, d_recv, e_send, e_recv, f_send, f_recv, h_send, h_recv, n_send, n_recv,
):
    tok, x, pb = lax.axis_index("tok"), lax.axis_index("feat"), lax.axis_index("pb")
    z, k = lax.div(tok, 2), lax.rem(pb, 2)
    y = lax.rem(tok, 2) * 2 + lax.div(pb, 2)
    home, z2 = lax.div(z, 2), lax.rem(z, 2)
    at_home = home == x

    def xs(d):
        return lax.rem(x + d, 4)

    def ys(d):
        return lax.rem(y + d, 4)

    x_dev = [None] + [place(xs(d), y, z, k) for d in (1, 2, 3)]
    y_dev = [None] + [place(x, ys(d), z, k) for d in (1, 2, 3)]
    twin = place(x, y, z, 1 - k)

    def local(src, dst, sem):
        return pltpu.make_async_copy(src, dst, sem)

    def remote(src, dst, send, recv, dev):
        return pltpu.make_async_remote_copy(
            src_ref=src, dst_ref=dst, send_sem=send, recv_sem=recv,
            device_id=dev, device_id_type=MESH,
        )

    sent, last = [], []

    def arrived(ref, sem):
        local(ref, ref, sem).wait()

    q_rows = pl.ds(pl.multiple_of(x * 32, 32), 32)
    load_q = [local(q.at[q_rows, :], qv.at[m], l_sem.at[m]) for m, q in enumerate((q_out, q_in))]
    for c in load_q:
        c.start()

    @pl.when(k == 0)
    def _():
        local(s_inv, mbuf.at[0], l_sem.at[2]).start()

    @pl.when(k == 1)
    def _():
        local(a_inv, mbuf.at[1], l_sem.at[2]).start()

    load_x = [local(t, xv.at[m], l_sem.at[3 + m]) for m, t in enumerate((grads, acts))]
    for c in load_x:
        c.start()

    barrier = pltpu.get_barrier_semaphore()

    def greet(dev):
        pl.semaphore_signal(barrier, inc=1, device_id=dev, device_id_type=MESH)

    def greet_source(i, carry):
        sx, sz, sk = lax.div(i, 4), 2 * x + lax.rem(lax.div(i, 2), 2), lax.rem(i, 2)
        me = (sx == x) & (sz == z) & (sk == k)

        @pl.when(jnp.logical_not(me))
        def _():
            greet(place(sx, y, sz, sk))

        return carry

    lax.fori_loop(0, 16, greet_source, 0)
    for dev in (y_dev[1], y_dev[3], x_dev[1], x_dev[2], x_dev[3], twin):
        greet(dev)

    lane = lax.broadcasted_iota(jnp.int32, (8, 128), 1)
    low = lax.broadcasted_iota(jnp.int32, (1, 128), 1) < 64

    def join(a, b):
        return jnp.where(low, a, b)

    def flip(a):
        return pltpu.roll(a, 64, 1)

    for c in load_q:
        c.wait()
    for m in range(2):
        for plane in range(4):
            col = [(plane + d) % 4 * 128 for d in range(4)]
            up, down = (qv[m, :, col[d]:col[d] + 128].astype(F32) for d in (1, 3))
            qrel[m, plane, 0] = qv[m, :, col[2]:col[2] + 128]
            qrel[m, plane, 1] = join(up, flip(down)).astype(BF16)
            qrel[m, plane, 2] = join(flip(up), down).astype(BF16)
            qrel[m, plane, 3] = qv[m, :, col[0]:col[0] + 128]

    arrived(mbuf.at[k], l_sem.at[2])
    mt[pl.ds(pl.multiple_of(k * 128, 128), 128), :] = mbuf[k].T
    pl.semaphore_wait(barrier, 22 - at_home.astype(jnp.int32))

    @pl.when(k == 0)
    def _():
        remote(a_inv, mbuf.at[0], m_send, m_recv, twin).start()

    @pl.when(k == 1)
    def _():
        remote(s_inv, mbuf.at[1], m_send, m_recv, twin).start()

    q_dst_rows = pl.ds(pl.multiple_of(k * 128 + x * 32, 32), 32)
    mine64 = pl.ds(pl.multiple_of(x * 64, 64), 64)
    mb = both.at[k]

    def ship(src, dst, send, recv, dev, to=sent):
        c = remote(src, dst, send, recv, dev)
        c.start()
        to.append(c)

    def a_copy(p, i):
        zt, kt = lax.rem(z + 4 + lax.div(i, 2), 8), lax.rem(i, 2)
        me = at_home & (zt == z) & (kt == k)
        src = qrel.at[kt, lax.div(zt, 2), p]
        dst = qg.at[p, z2, y, q_dst_rows, :]
        far = remote(src, dst, a_send.at[p, i], a_recv.at[p], place(home, y, zt, kt))
        return me, local(src, dst, a_recv.at[p]), far

    def d_copy(p, i):
        zt = lax.rem(z + 4 + i, 8)
        me = at_home & (zt == z)
        dst = mb.at[p, z2, y, mine64, :]
        far = remote(lq.at[p], dst, d_send.at[p, i], d_recv.at[p], place(home, y, zt, k))
        return me, local(lq.at[p], dst, d_recv.at[p]), far

    def fan_start(copy, count, p):
        def step(i, carry):
            me, near_copy, far = copy(p, i)

            @pl.when(me)
            def _():
                near_copy.start()

            @pl.when(jnp.logical_not(me))
            def _():
                far.start()

            return carry

        lax.fori_loop(0, count, step, 0)

    def fan_sent(copy, count, p):
        def step(i, carry):
            me, _, far = copy(p, i)

            @pl.when(jnp.logical_not(me))
            def _():
                far.wait_send()

            return carry

        lax.fori_loop(0, count, step, 0)

    def spread(buf, p, send, recv):
        for half, side, d in ((0, 0, 1), (1, 1, 3), (1, 0, 1), (0, 1, 3)):
            mine = buf.at[p, half, y]
            ship(mine, mine, send.at[p, side, half], recv.at[p, side, half], y_dev[d])

    def near_half(buf, p, recv, side, half):
        b = ys(3) if side == 0 else ys(1)
        arrived(buf.at[p, half, b], recv.at[p, side, half])

    def pass_on(buf, p, send, recv):
        for side, d in ((0, 1), (1, 3)):
            near_half(buf, p, recv, side, side)
            half = buf.at[p, side, ys(3) if side == 0 else ys(1)]
            ship(half, half, send.at[p, 2, side], recv.at[p, 2, side], y_dev[d])

    def far_half(buf, p, recv, side):
        arrived(buf.at[p, side, ys(2)], recv.at[p, 2, side])

    def to_twin(p, b, half):
        block = mb.at[p, half, ys(b)]
        ship(block, block, f_send.at[p, b, half], f_recv.at[p, b, half], twin)

    def A(p):
        fan_start(a_copy, 16, p)

    def A_sent(p):
        fan_sent(a_copy, 16, p)

    def B(p):
        arrived(qg.at[p, :, y], a_recv.at[p])
        spread(qg, p, b_send, b_recv)

    def B2(p):
        pass_on(qg, p, b_send, b_recv)

    def C(p):
        for side in range(2):
            near_half(qg, p, b_recv, side, 1 - side)
            far_half(qg, p, b_recv, side)
        part[p] = jnp.dot(mt[...], qg[p].reshape(2048, 128), preferred_element_type=F32)
        for d in (1, 2, 3):
            rows = pl.ds(pl.multiple_of(xs(d) * 64, 64), 64)
            ship(part.at[p, rows, :], cbuf.at[p, d - 1], c_send.at[p, d - 1],
                 c_recv.at[p, d - 1], x_dev[d])

    def D(p):
        for d in range(3):
            arrived(cbuf.at[p, d], c_recv.at[p, d])
        total = part[p, mine64, :] + cbuf[p, 0] + cbuf[p, 1] + cbuf[p, 2]
        lq[p] = total.astype(BF16)
        fan_start(d_copy, 8, p)

    def E(p):
        arrived(mb.at[p, :, y], d_recv.at[p])
        spread(mb, p, e_send, e_recv)
        to_twin(p, 0, 0)
        to_twin(p, 0, 1)

    def E2(p):
        pass_on(mb, p, e_send, e_recv)
        to_twin(p, 3, 0)
        to_twin(p, 1, 1)

    def E3(p):
        for side in range(2):
            near_half(mb, p, e_recv, side, 1 - side)
            to_twin(p, 3 if side == 0 else 1, 1 - side)
        for side in range(2):
            far_half(mb, p, e_recv, side)
            to_twin(p, 2, side)

    def factor():
        c = 1 - k
        arrived(mbuf.at[c], m_recv)
        mt[pl.ds(pl.multiple_of(c * 128, 128), 128), :] = mbuf[c].T

    def acts_in():
        for c in load_x:
            c.wait()

    def twin_in(p):
        for b in range(4):
            for half in range(2):
                arrived(both.at[1 - k, p, half, ys(b)], f_recv.at[p, b, half])

    def tiles(half, body):
        def step(i, carry):
            rows = pl.ds(pl.multiple_of((i + half * (HALF // TILE)) * TILE, TILE), TILE)
            body(rows, pl.ds(pl.multiple_of(i * TILE, TILE), TILE))
            return carry

        lax.fori_loop(0, HALF // TILE, step, 0)

    def project(p, m, rows):
        w = both[m, p].reshape(2048, 128)
        return jnp.dot(xv[m, rows, :], w, preferred_element_type=F32)

    def sides(turn):
        return k if turn == 0 else 1 - k

    def H0(turn):
        m = sides(turn)
        for half in range(2):
            def body(rows, inner):
                opp[m, rows, :] = project(0, m, rows).astype(BF16)

            tiles(half, body)
            side, d = ((1, 3), (0, 1))[half]
            ship(opp.at[m, pl.ds(HALF * half, HALF), :], hrecv.at[side, m],
                 h_send.at[turn, side], h_recv.at[m, side], x_dev[d])

    def to_neighbour(s, half, j):
        rows = pl.ds(HALF * half, HALF)
        ship(near.at[j, s, rows, :], frecv.at[j, s, rows, :], n_send.at[s, half, j],
             n_recv.at[s, half, j], x_dev[1 if j == 0 else 3], last)

    def H1(s, half):
        def body(rows, inner):
            g, a = (project(s + 1, m, rows) for m in range(2))
            both_ways = join(g, flip(a)), join(flip(g), a)
            near[half, s, rows, :] = both_ways[half].astype(BF16)
            pend[s, half, inner, :] = both_ways[1 - half]

        tiles(half, body)
        to_neighbour(s, half, half)

    def H2(s, half):
        j = 1 - half
        if s == 0:
            for m in range(2):
                arrived(hrecv.at[j, m], h_recv.at[m, j])

        def body(rows, inner):
            g, a = (hrecv[j, m, inner, :].astype(F32) for m in range(2))
            more = join(g, flip(a)) if s == 0 else join(flip(g), a)
            near[j, s, rows, :] = (pend[s, half, inner, :] + more).astype(BF16)

        tiles(half, body)
        to_neighbour(s, half, j)

    def H3(turn):
        m = sides(turn)
        for half in range(2):
            def body(rows, inner):
                own[m, rows, :] = project(3, m, rows)

            tiles(half, body)

    query = lax.broadcasted_iota(jnp.int32, (8, 128), 0)
    pick = jnp.where(lax.div(lane, RANK) == query, 1.0, 0.0).astype(F32)

    def scores(half):
        rows = pl.ds(HALF * half, HALF)
        for s in range(2):
            for j in range(2):
                arrived(frecv.at[j, s, rows, :], n_recv.at[s, half, j])
        first, last = (frecv[0, s, rows, :].astype(F32) + frecv[1, s, rows, :].astype(F32)
                       for s in range(2))
        g = own[0, rows, :] + join(first, flip(last))
        a = own[1, rows, :] + join(flip(first), last)
        prod = g * a
        out[:, rows] = lax.dot_general(
            pick, prod, (((1,), (1,)), ((), ())),
            precision=lax.Precision.HIGHEST, preferred_element_type=F32,
        )

    A(0)
    factor()
    fan_sent(a_copy, 16, 0)
    A(1)
    fan_sent(a_copy, 16, 1)
    A(2)
    B(0)
    B2(0)
    B(1)
    fan_sent(a_copy, 16, 2)
    A(3)
    C(0)
    B2(1)
    B(2)
    D(0)
    C(1)
    B2(2)
    B(3)
    D(1)
    C(2)
    B2(3)
    E(0)
    D(2)
    C(3)
    E2(0)
    E(1)
    D(3)
    E3(0)
    E2(1)
    E(2)
    acts_in()
    H0(0)
    twin_in(0)
    H0(1)
    E3(1)
    E(3)
    E2(2)
    twin_in(1)
    H1(0,0)
    H1(0,1)
    E3(2)
    E2(3)
    H2(0,0)
    H2(0,1)
    twin_in(2)
    H1(1,0)
    H1(1,1)
    H2(1,0)
    H2(1,1)
    E3(3)
    H3(0)
    twin_in(3)
    H3(1)
    for c in sent:
        c.wait_send()
    remote(mbuf.at[k], mbuf.at[k], m_send, m_recv, twin).wait_send()
    fan_sent(a_copy, 16, 3)
    for p in range(4):
        fan_sent(d_copy, 8, p)

    scores(0)
    scores(1)

    for c in last:
        c.wait_send()


def per_device(out_grads, acts, s_inverse, a_inverse, query_out, query_in):
    dma = pltpu.SemaphoreType.DMA
    vmem = pltpu.VMEM
    summed = pl.pallas_call(
        kernel,
        out_shape=jax.ShapeDtypeStruct((8, ROWS), F32),
        in_specs=[pl.BlockSpec(memory_space=pl.ANY)] * 6,
        out_specs=pl.BlockSpec(memory_space=pltpu.VMEM),
        scratch_shapes=[
            vmem((2, ROWS, 2048), BF16),
            vmem((2, 2048, 128), BF16),
            vmem((256, 2048), BF16),
            vmem((2, 32, 512), BF16),
            vmem((2, 4, 4, 32, 128), BF16),
            vmem((4, 2, 4, 256, 128), BF16),
            vmem((4, 256, 128), F32),
            vmem((4, 3, 64, 128), F32),
            vmem((4, 64, 128), BF16),
            vmem((2, 4, 2, 4, 256, 128), BF16),
            vmem((2, ROWS, 128), F32),
            vmem((2, ROWS, 128), BF16),
            vmem((2, 2, ROWS, 128), BF16),
            vmem((2, 2, HALF, 128), BF16),
            vmem((2, 2, ROWS, 128), BF16),
            vmem((2, 2, HALF, 128), F32),
            dma((5,)), dma, dma, dma((4, 16)), dma((4,)), dma((4, 3, 2)), dma((4, 3, 2)),
            dma((4, 3)), dma((4, 3)), dma((4, 8)), dma((4,)), dma((4, 3, 2)), dma((4, 3, 2)),
            dma((4, 4, 2)), dma((4, 4, 2)), dma((2, 2)), dma((2, 2)), dma((2, 2, 2)), dma((2, 2, 2)),
        ],
        compiler_params=pltpu.CompilerParams(
            collective_id=0, has_side_effects=True, vmem_limit_bytes=62 * 1024 * 1024
        ),
    )(out_grads, acts, s_inverse, a_inverse, query_out, query_in)
    return summed * (1.0 / RANK**0.5)


def solution(mesh):
    placed = (
        P(("tok", "pb"), "feat"),
        P(("tok", "pb"), "feat"),
        P("feat", ("tok", "pb")),
        P("feat", ("tok", "pb")),
        P(("tok", "pb"), None),
        P(("tok", "pb"), None),
    )
    return jax.shard_map(
        per_device, mesh=mesh, in_specs=placed, out_specs=P("feat", ("tok", "pb")), check_vma=False
    )
```

```python
import jax
import jax.numpy as jnp
from jax import lax
from jax.experimental import pallas as pl
from jax.experimental.pallas import tpu as pltpu
from jax.sharding import PartitionSpec as P

RANK = 16
MESH = pl.DeviceIdType.MESH
BF16, F32 = jnp.bfloat16, jnp.float32
ROWS = 1280
HALF = ROWS // 2
TILE = 640


def place(x, y, z, k):
    return (z * 2 + lax.div(y, 2), x, lax.rem(y, 2) * 2 + k)


def kernel(
    grads, acts, s_inv, a_inv, q_out, q_in, out,
    xv, mbuf, mt, qv, qrel, qg, part, cbuf, lq, both, own, opp, near, hrecv, frecv, pend,
    l_sem, m_send, m_recv, a_send, a_recv, b_send, b_recv, c_send, c_recv,
    d_send, d_recv, e_send, e_recv, f_send, f_recv, h_send, h_recv, n_send, n_recv,
):
    tok, x, pb = lax.axis_index("tok"), lax.axis_index("feat"), lax.axis_index("pb")
    z, k = lax.div(tok, 2), lax.rem(pb, 2)
    y = lax.rem(tok, 2) * 2 + lax.div(pb, 2)
    home, z2 = lax.div(z, 2), lax.rem(z, 2)
    at_home = home == x

    def xs(d):
        return lax.rem(x + d, 4)

    def ys(d):
        return lax.rem(y + d, 4)

    x_dev = [None] + [place(xs(d), y, z, k) for d in (1, 2, 3)]
    y_dev = [None] + [place(x, ys(d), z, k) for d in (1, 2, 3)]
    twin = place(x, y, z, 1 - k)

    def local(src, dst, sem):
        return pltpu.make_async_copy(src, dst, sem)

    def remote(src, dst, send, recv, dev):
        return pltpu.make_async_remote_copy(
            src_ref=src, dst_ref=dst, send_sem=send, recv_sem=recv,
            device_id=dev, device_id_type=MESH,
        )

    sent, last = [], []

    def arrived(ref, sem):
        local(ref, ref, sem).wait()

    q_rows = pl.ds(pl.multiple_of(x * 32, 32), 32)
    load_q = [local(q.at[q_rows, :], qv.at[m], l_sem.at[m]) for m, q in enumerate((q_out, q_in))]
    for c in load_q:
        c.start()

    @pl.when(k == 0)
    def _():
        local(s_inv, mbuf.at[0], l_sem.at[2]).start()

    @pl.when(k == 1)
    def _():
        local(a_inv, mbuf.at[1], l_sem.at[2]).start()

    load_x = [local(t, xv.at[m], l_sem.at[3 + m]) for m, t in enumerate((grads, acts))]
    for c in load_x:
        c.start()

    barrier = pltpu.get_barrier_semaphore()

    def greet(dev):
        pl.semaphore_signal(barrier, inc=1, device_id=dev, device_id_type=MESH)

    def greet_source(i, carry):
        sx, sz, sk = lax.div(i, 4), 2 * x + lax.rem(lax.div(i, 2), 2), lax.rem(i, 2)
        me = (sx == x) & (sz == z) & (sk == k)

        @pl.when(jnp.logical_not(me))
        def _():
            greet(place(sx, y, sz, sk))

        return carry

    lax.fori_loop(0, 16, greet_source, 0)
    for dev in (y_dev[1], y_dev[3], x_dev[1], x_dev[2], x_dev[3], twin):
        greet(dev)

    lane = lax.broadcasted_iota(jnp.int32, (8, 128), 1)
    low = lax.broadcasted_iota(jnp.int32, (1, 128), 1) < 64

    def join(a, b):
        return jnp.where(low, a, b)

    def flip(a):
        return pltpu.roll(a, 64, 1)

    for c in load_q:
        c.wait()
    for m in range(2):
        for plane in range(4):
            col = [(plane + d) % 4 * 128 for d in range(4)]
            up, down = (qv[m, :, col[d]:col[d] + 128].astype(F32) for d in (1, 3))
            qrel[m, plane, 0] = qv[m, :, col[2]:col[2] + 128]
            qrel[m, plane, 1] = join(up, flip(down)).astype(BF16)
            qrel[m, plane, 2] = join(flip(up), down).astype(BF16)
            qrel[m, plane, 3] = qv[m, :, col[0]:col[0] + 128]

    arrived(mbuf.at[k], l_sem.at[2])
    mt[pl.ds(pl.multiple_of(k * 128, 128), 128), :] = mbuf[k].T
    pl.semaphore_wait(barrier, 22 - at_home.astype(jnp.int32))

    @pl.when(k == 0)
    def _():
        remote(a_inv, mbuf.at[0], m_send, m_recv, twin).start()

    @pl.when(k == 1)
    def _():
        remote(s_inv, mbuf.at[1], m_send, m_recv, twin).start()

    q_dst_rows = pl.ds(pl.multiple_of(k * 128 + x * 32, 32), 32)
    mine64 = pl.ds(pl.multiple_of(x * 64, 64), 64)
    mb = both.at[k]

    def ship(src, dst, send, recv, dev, to=sent):
        c = remote(src, dst, send, recv, dev)
        c.start()
        to.append(c)

    def a_copy(p, i):
        zt, kt = lax.rem(z + 4 + lax.div(i, 2), 8), lax.rem(i, 2)
        me = at_home & (zt == z) & (kt == k)
        src = qrel.at[kt, lax.div(zt, 2), p]
        dst = qg.at[p, z2, y, q_dst_rows, :]
        far = remote(src, dst, a_send.at[p, i], a_recv.at[p], place(home, y, zt, kt))
        return me, local(src, dst, a_recv.at[p]), far

    def d_copy(p, i):
        zt = lax.rem(z + 4 + i, 8)
        me = at_home & (zt == z)
        dst = mb.at[p, z2, y, mine64, :]
        far = remote(lq.at[p], dst, d_send.at[p, i], d_recv.at[p], place(home, y, zt, k))
        return me, local(lq.at[p], dst, d_recv.at[p]), far

    def fan_start(copy, count, p):
        def step(i, carry):
            me, near_copy, far = copy(p, i)

            @pl.when(me)
            def _():
                near_copy.start()

            @pl.when(jnp.logical_not(me))
            def _():
                far.start()

            return carry

        lax.fori_loop(0, count, step, 0)

    def fan_sent(copy, count, p):
        def step(i, carry):
            me, _, far = copy(p, i)

            @pl.when(jnp.logical_not(me))
            def _():
                far.wait_send()

            return carry

        lax.fori_loop(0, count, step, 0)

    def spread(buf, p, send, recv):
        for half, side, d in ((0, 0, 1), (1, 1, 3), (1, 0, 1), (0, 1, 3)):
            mine = buf.at[p, half, y]
            ship(mine, mine, send.at[p, side, half], recv.at[p, side, half], y_dev[d])

    def near_half(buf, p, recv, side, half):
        b = ys(3) if side == 0 else ys(1)
        arrived(buf.at[p, half, b], recv.at[p, side, half])

    def pass_on(buf, p, send, recv):
        for side, d in ((0, 1), (1, 3)):
            near_half(buf, p, recv, side, side)
            half = buf.at[p, side, ys(3) if side == 0 else ys(1)]
            ship(half, half, send.at[p, 2, side], recv.at[p, 2, side], y_dev[d])

    def far_half(buf, p, recv, side):
        arrived(buf.at[p, side, ys(2)], recv.at[p, 2, side])

    def to_twin(p, b, half):
        block = mb.at[p, half, ys(b)]
        ship(block, block, f_send.at[p, b, half], f_recv.at[p, b, half], twin)

    def A(p):
        fan_start(a_copy, 16, p)

    def A_sent(p):
        fan_sent(a_copy, 16, p)

    def B(p):
        arrived(qg.at[p, :, y], a_recv.at[p])
        spread(qg, p, b_send, b_recv)

    def B2(p):
        pass_on(qg, p, b_send, b_recv)

    def C(p):
        for side in range(2):
            near_half(qg, p, b_recv, side, 1 - side)
            far_half(qg, p, b_recv, side)
        part[p] = jnp.dot(mt[...], qg[p].reshape(2048, 128), preferred_element_type=F32)
        for d in (1, 2, 3):
            rows = pl.ds(pl.multiple_of(xs(d) * 64, 64), 64)
            ship(part.at[p, rows, :], cbuf.at[p, d - 1], c_send.at[p, d - 1],
                 c_recv.at[p, d - 1], x_dev[d])

    def D(p):
        for d in range(3):
            arrived(cbuf.at[p, d], c_recv.at[p, d])
        total = part[p, mine64, :] + cbuf[p, 0] + cbuf[p, 1] + cbuf[p, 2]
        lq[p] = total.astype(BF16)
        fan_start(d_copy, 8, p)

    def E(p):
        arrived(mb.at[p, :, y], d_recv.at[p])
        spread(mb, p, e_send, e_recv)
        to_twin(p, 0, 0)
        to_twin(p, 0, 1)

    def E2(p):
        pass_on(mb, p, e_send, e_recv)
        to_twin(p, 3, 0)
        to_twin(p, 1, 1)

    def E3(p):
        for side in range(2):
            near_half(mb, p, e_recv, side, 1 - side)
            to_twin(p, 3 if side == 0 else 1, 1 - side)
        for side in range(2):
            far_half(mb, p, e_recv, side)
            to_twin(p, 2, side)

    def factor():
        c = 1 - k
        arrived(mbuf.at[c], m_recv)
        mt[pl.ds(pl.multiple_of(c * 128, 128), 128), :] = mbuf[c].T

    def acts_in():
        for c in load_x:
            c.wait()

    def twin_in(p):
        for b in range(4):
            for half in range(2):
                arrived(both.at[1 - k, p, half, ys(b)], f_recv.at[p, b, half])

    def tiles(half, body):
        def step(i, carry):
            rows = pl.ds(pl.multiple_of((i + half * (HALF // TILE)) * TILE, TILE), TILE)
            body(rows, pl.ds(pl.multiple_of(i * TILE, TILE), TILE))
            return carry

        lax.fori_loop(0, HALF // TILE, step, 0)

    def project(p, m, rows):
        w = both[m, p].reshape(2048, 128)
        return jnp.dot(xv[m, rows, :], w, preferred_element_type=F32)

    def sides(turn):
        return k if turn == 0 else 1 - k

    def H0(turn):
        m = sides(turn)
        opp[m] = project(0, m, pl.ds(0, ROWS)).astype(BF16)
        for half in range(2):
            side, d = ((1, 3), (0, 1))[half]
            ship(opp.at[m, pl.ds(HALF * half, HALF), :], hrecv.at[side, m],
                 h_send.at[turn, side], h_recv.at[m, side], x_dev[d])

    def to_neighbour(s, half, j):
        rows = pl.ds(HALF * half, HALF)
        ship(near.at[j, s, rows, :], frecv.at[j, s, rows, :], n_send.at[s, half, j],
             n_recv.at[s, half, j], x_dev[1 if j == 0 else 3], last)

    def H1(s, half):
        def body(rows, inner):
            g, a = (project(s + 1, m, rows) for m in range(2))
            both_ways = join(g, flip(a)), join(flip(g), a)
            near[half, s, rows, :] = both_ways[half].astype(BF16)
            pend[s, half, inner, :] = both_ways[1 - half]

        tiles(half, body)
        to_neighbour(s, half, half)

    def H2(s, half):
        j = 1 - half
        if s == 0:
            for m in range(2):
                arrived(hrecv.at[j, m], h_recv.at[m, j])

        def body(rows, inner):
            g, a = (hrecv[j, m, inner, :].astype(F32) for m in range(2))
            more = join(g, flip(a)) if s == 0 else join(flip(g), a)
            near[j, s, rows, :] = (pend[s, half, inner, :] + more).astype(BF16)

        tiles(half, body)
        to_neighbour(s, half, j)

    def H3(turn):
        m = sides(turn)
        for half in range(2):
            def body(rows, inner):
                own[m, rows, :] = project(3, m, rows)

            tiles(half, body)

    query = lax.broadcasted_iota(jnp.int32, (8, 128), 0)
    pick = jnp.where(lax.div(lane, RANK) == query, 1.0, 0.0).astype(F32)

    def scores(half):
        rows = pl.ds(HALF * half, HALF)
        for s in range(2):
            for j in range(2):
                arrived(frecv.at[j, s, rows, :], n_recv.at[s, half, j])
        first, last = (frecv[0, s, rows, :].astype(F32) + frecv[1, s, rows, :].astype(F32)
                       for s in range(2))
        g = own[0, rows, :] + join(first, flip(last))
        a = own[1, rows, :] + join(flip(first), last)
        prod = g * a
        out[:, rows] = lax.dot_general(
            pick, prod, (((1,), (1,)), ((), ())),
            precision=lax.Precision.HIGHEST, preferred_element_type=F32,
        )

    A(0)
    factor()
    fan_sent(a_copy, 16, 0)
    A(1)
    fan_sent(a_copy, 16, 1)
    A(2)
    B(0)
    B2(0)
    B(1)
    fan_sent(a_copy, 16, 2)
    A(3)
    C(0)
    B2(1)
    B(2)
    D(0)
    C(1)
    B2(2)
    B(3)
    D(1)
    C(2)
    B2(3)
    E(0)
    D(2)
    C(3)
    E2(0)
    E(1)
    D(3)
    E3(0)
    E2(1)
    E(2)
    acts_in()
    H0(0)
    twin_in(0)
    H0(1)
    E3(1)
    E(3)
    E2(2)
    twin_in(1)
    H1(0,0)
    H1(0,1)
    E3(2)
    E2(3)
    H2(0,0)
    H2(0,1)
    twin_in(2)
    H1(1,0)
    H1(1,1)
    H2(1,0)
    H2(1,1)
    E3(3)
    H3(0)
    twin_in(3)
    H3(1)
    for c in sent:
        c.wait_send()
    remote(mbuf.at[k], mbuf.at[k], m_send, m_recv, twin).wait_send()
    fan_sent(a_copy, 16, 3)
    for p in range(4):
        fan_sent(d_copy, 8, p)

    scores(0)
    scores(1)

    for c in last:
        c.wait_send()


def per_device(out_grads, acts, s_inverse, a_inverse, query_out, query_in):
    dma = pltpu.SemaphoreType.DMA
    vmem = pltpu.VMEM
    summed = pl.pallas_call(
        kernel,
        out_shape=jax.ShapeDtypeStruct((8, ROWS), F32),
        in_specs=[pl.BlockSpec(memory_space=pl.ANY)] * 6,
        out_specs=pl.BlockSpec(memory_space=pltpu.VMEM),
        scratch_shapes=[
            vmem((2, ROWS, 2048), BF16),
            vmem((2, 2048, 128), BF16),
            vmem((256, 2048), BF16),
            vmem((2, 32, 512), BF16),
            vmem((2, 4, 4, 32, 128), BF16),
            vmem((4, 2, 4, 256, 128), BF16),
            vmem((4, 256, 128), F32),
            vmem((4, 3, 64, 128), F32),
            vmem((4, 64, 128), BF16),
            vmem((2, 4, 2, 4, 256, 128), BF16),
            vmem((2, ROWS, 128), F32),
            vmem((2, ROWS, 128), BF16),
            vmem((2, 2, ROWS, 128), BF16),
            vmem((2, 2, HALF, 128), BF16),
            vmem((2, 2, ROWS, 128), BF16),
            vmem((2, 2, HALF, 128), F32),
            dma((5,)), dma, dma, dma((4, 16)), dma((4,)), dma((4, 3, 2)), dma((4, 3, 2)),
            dma((4, 3)), dma((4, 3)), dma((4, 8)), dma((4,)), dma((4, 3, 2)), dma((4, 3, 2)),
            dma((4, 4, 2)), dma((4, 4, 2)), dma((2, 2)), dma((2, 2)), dma((2, 2, 2)), dma((2, 2, 2)),
        ],
        compiler_params=pltpu.CompilerParams(
            collective_id=0, has_side_effects=True, vmem_limit_bytes=62 * 1024 * 1024
        ),
    )(out_grads, acts, s_inverse, a_inverse, query_out, query_in)
    return summed * (1.0 / RANK**0.5)


def solution(mesh):
    placed = (
        P(("tok", "pb"), "feat"),
        P(("tok", "pb"), "feat"),
        P("feat", ("tok", "pb")),
        P("feat", ("tok", "pb")),
        P(("tok", "pb"), None),
        P(("tok", "pb"), None),
    )
    return jax.shard_map(
        per_device, mesh=mesh, in_specs=placed, out_specs=P("feat", ("tok", "pb")), check_vma=False
    )
```
